128 devices in a mesh: gx: 32 (over z, x, core), gy: 4 (over y).
Axes of the slice: x: 4, y: 4, z: 4, core: 2. Of those that a mesh axis runs over, the one named last changes fastest.
Arguments:
- leaf_maps: float32 [1, 4096, 32768], P(None, 'gy', 'gx'), may hold values from -5 to 14, as said below
Outputs:
- quad_maps: float32 [1, 4096, 32768], P(None, 'gy', 'gx')
The draws below stay inside these ranges and needn't reach their ends.
Inputs may be any that keep to these rules, and one draw needn't show every extreme that they name: `leaf_maps`: every patch's block is symmetric and positive definite.
All inputs are finite; a program needn't handle non-finite values.
Results may differ from the reference program's by a relative error of at most 0.000067.
Values sent between devices are 32-bit elements; how exact they have to be, the bound alone decides.
A program may use at most 128 MiB of HBM per device.

```python
import math
import jax
import jax.numpy as jnp
from jax import lax

E = 256
FIELDS = 1
ROWS = 4096
COLS = 32768
N_GX = 32
N_GY = 4


def draw_leaf_maps(key, part):
    side_cells = 4 * E
    blocks_y = ROWS // side_cells
    blocks_x = COLS // side_cells
    block_count = FIELDS * blocks_y * blocks_x

    def one_block(index):
        block_key = jax.random.fold_in(key, index)
        factor_key, scale_key = jax.random.split(block_key)
        factor = jnp.clip(jax.random.normal(factor_key, (side_cells, side_cells), jnp.float32), -6.0, 6.0)
        scales = jnp.exp(jax.random.uniform(scale_key, (side_cells,), jnp.float32, 0.0, math.log(1.5)))
        gram = jnp.dot(factor, factor.T, precision=lax.Precision.HIGHEST) / float(side_cells)
        gram = 0.5 * (gram + gram.T)
        shifted = scales[:, None] * gram * scales[None, :]
        return shifted + 0.25 * jnp.eye(side_cells, dtype=jnp.float32)
    blocks = lax.map(one_block, jnp.arange(block_count, dtype=jnp.int32))
    blocks = blocks.reshape(FIELDS, blocks_y, blocks_x, side_cells, side_cells).transpose(0, 1, 3, 2, 4)
    return blocks.reshape(FIELDS, ROWS, COLS).astype(jnp.float32)


def setup_inputs(seed: int = 0) -> dict:
    splits = jax.random.split(jax.random.key(seed), 2)
    leaf_maps = draw_leaf_maps(jax.random.fold_in(splits[1], 71), 0)
    return dict(leaf_maps=leaf_maps)


def pick_rows(matrix, labels, row_labels, edge_width):
    return jnp.concatenate([matrix[:, labels.index(label_id) * edge_width:(labels.index(label_id) + 1) * edge_width, :] for label_id in row_labels], axis=1)

def pick_cols(matrix, labels, col_labels, edge_width):
    return jnp.concatenate([matrix[:, :, labels.index(label_id) * edge_width:(labels.index(label_id) + 1) * edge_width] for label_id in col_labels], axis=2)

def merge(first_map, first_labels, second_map, second_labels, shared, out_order, edge_width):
    coupling = pick_cols(pick_rows(first_map, first_labels, shared, edge_width), first_labels, shared, edge_width)
    coupling = coupling + pick_cols(pick_rows(second_map, second_labels, shared, edge_width), second_labels, shared, edge_width)
    pieces = []
    direct_rows = []
    for label_id in out_order:
        if label_id in first_labels:
            source, source_labels = (first_map, first_labels)
        else:
            source, source_labels = (second_map, second_labels)
        row_band = pick_rows(source, source_labels, [label_id], edge_width)
        pieces.append(pick_cols(row_band, source_labels, shared, edge_width))
        blocks = []
        for other_id in out_order:
            if other_id in source_labels:
                blocks.append(pick_cols(row_band, source_labels, [other_id], edge_width))
            else:
                blocks.append(jnp.zeros((row_band.shape[0], edge_width, edge_width), jnp.float32))
        direct_rows.append(jnp.concatenate(blocks, axis=2))
    edge_rows = jnp.concatenate(pieces, axis=1)
    direct = jnp.concatenate(direct_rows, axis=1)
    factor = jnp.linalg.cholesky(coupling)
    half_way = jax.scipy.linalg.solve_triangular(factor, jnp.swapaxes(edge_rows, 1, 2), lower=True)
    solved = jax.scipy.linalg.solve_triangular(factor, half_way, lower=True, trans=1)
    return direct - jnp.einsum('fik,fkj->fij', edge_rows, solved, precision=lax.Precision.HIGHEST)

def quad_map(quad_block):
    patch_len = 4 * E

    def leaf_at(x_pos, y_pos):
        return quad_block[:, y_pos * patch_len:(y_pos + 1) * patch_len, x_pos * patch_len:(x_pos + 1) * patch_len]
    low_pair = merge(leaf_at(0, 0), [0, 9, 2, 3], leaf_at(1, 0), [9, 1, 4, 5], [9], [0, 1, 2, 4, 3, 5], E)
    high_pair = merge(leaf_at(0, 1), [0, 9, 2, 3], leaf_at(1, 1), [9, 1, 4, 5], [9], [0, 1, 2, 4, 3, 5], E)
    return merge(low_pair, [0, 2, 4, 5, 10, 11], high_pair, [1, 3, 10, 11, 6, 7], [10, 11], [0, 2, 4, 5, 1, 3, 6, 7], E)

def reference(leaf_maps):
    patch_len = 4 * E
    half_rows = N_GY // 2
    half_cols = N_GX // 2
    all_quads = leaf_maps.reshape(FIELDS, 2, half_rows, patch_len, 2, half_cols, patch_len)
    all_quads = all_quads.transpose(2, 5, 0, 1, 3, 4, 6).reshape(half_rows * half_cols, FIELDS, 2 * patch_len, 2 * patch_len)
    merged = lax.map(quad_map, all_quads)
    merged = merged.reshape(half_rows, half_cols, FIELDS, 2, patch_len, 2, patch_len).transpose(2, 3, 0, 4, 5, 1, 6)
    return merged.reshape(FIELDS, ROWS, COLS)
```

```python
import functools

import jax
import jax.numpy as jnp
from jax import lax
from jax.experimental import pallas as pl
from jax.experimental.pallas import tpu as pltpu
from jax.sharding import PartitionSpec as P

F32 = jnp.float32
BF16 = jnp.bfloat16
B = 128
W = 4


def partner_2(value, axis, apart):
    mask = 2**apart
    pairs = [(source, source ^ mask) for source in range(lax.axis_size(axis))]
    return lax.ppermute(value, axis, pairs)


def small_inverse(s):
    def get(d, i, j):
        return d[(max(i, j), min(i, j))]

    s = dict(s)
    for k in range(0, W, 2):
        pair = (k, k + 1)
        a, b, c = get(s, k, k), get(s, k + 1, k), get(s, k + 1, k + 1)
        r = 1.0 / (a * c - b * b)
        t0, t1 = {}, {}
        for i in range(W):
            if i not in pair:
                x, y = get(s, i, k), get(s, i, k + 1)
                t0[i] = (x * c - y * b) * r
                t1[i] = (y * a - x * b) * r
        block = {(0, 0): -c * r, (1, 0): b * r, (1, 1): -a * r}
        new = {}
        for i in range(W):
            for j in range(i + 1):
                if i in pair and j in pair:
                    new[(i, j)] = block[(i - k, j - k)]
                elif i in pair:
                    new[(i, j)] = (t0 if i == k else t1)[j]
                elif j in pair:
                    new[(i, j)] = (t0 if j == k else t1)[i]
                else:
                    new[(i, j)] = get(s, i, j) - (get(s, i, k) * t0[j] + get(s, i, k + 1) * t1[j])
        s = new
    return {key: -value for key, value in s.items()}


def sweep(mats):
    lane = lax.broadcasted_iota(jnp.int32, (8, B), 1)
    sub = lax.broadcasted_iota(jnp.int32, (8, B), 0)
    tiles = B // 8
    mats = [[m[t * 8 : (t + 1) * 8, :] for t in range(tiles)] for m in mats]

    def over_lanes(tile, c):
        return jnp.broadcast_to(tile[:, c : c + 1], (8, B))

    def over_rows(tile, r):
        return jnp.broadcast_to(tile[r : r + 1, :], (8, B))

    for k in range(0, B, W):
        kt, kr = k // 8, k % 8
        inside = (lane >= k) & (lane < k + W)
        for index, a in enumerate(mats):
            cols = [[over_lanes(a[t], k + j) for t in range(tiles)] for j in range(W)]
            s = {(i, j): over_rows(cols[j][kt], kr + i) for i in range(W) for j in range(i + 1)}
            m = small_inverse(s)
            rows = [over_rows(a[kt], kr + j) for j in range(W)]
            solved = []
            for i in range(W):
                row = [m[(max(i, j), min(i, j))] for j in range(W)]
                acc = row[0] * rows[0]
                for j in range(1, W):
                    acc = acc + row[j] * rows[j]
                for j in range(W):
                    acc = jnp.where(lane == k + j, -row[j], acc)
                solved.append(acc)
            new = []
            for t in range(tiles):
                update = cols[0][t] * solved[0]
                for i in range(1, W):
                    update = update + cols[i][t] * solved[i]
                value = jnp.where(inside, 0.0, a[t]) - update
                if t == kt:
                    for i in range(W):
                        value = jnp.where(sub == kr + i, solved[i], value)
                new.append(value)
            mats[index] = new
    return [jnp.concatenate(m, axis=0) for m in mats]


def dot_full(a, b):
    return jnp.dot(a, b, precision=lax.Precision.HIGHEST, preferred_element_type=F32)


def block_inverse(mats, n):
    mats = [dict(m) for m in mats]
    for k in range(n):
        swept = sweep([m[(k, k)] for m in mats])
        others = [(k + 1 + i) % n for i in range(n - 1)]
        for m, minus in zip(mats, swept):
            p = -minus
            row = {j: m[(k, j)] for j in others}
            col = {i: m[(i, k)] for i in others}
            solved = {j: dot_full(p, row[j]) for j in others}
            for j in others:
                for i in others:
                    m[(i, j)] = m[(i, j)] - dot_full(col[i], solved[j])
            for j in others:
                m[(k, j)] = solved[j]
                m[(j, k)] = dot_full(col[j], p)
            m[(k, k)] = minus
    return [{key: -value for key, value in m.items()} for m in mats]


def split(x):
    hi = x.astype(BF16)
    return hi, (x - hi.astype(F32)).astype(BF16)


def dot_split(a, b, transposed=False):
    dims = (((1,), (1 if transposed else 0,)), ((), ()))
    one = functools.partial(lax.dot_general, dimension_numbers=dims, preferred_element_type=F32)
    return one(a[0], b[0]) + (one(a[0], b[1]) + one(a[1], b[0]))


def pack_inner_kernel(idx, hh_in, vv_in, hv_in, hh, vh):
    hh[...] = hh_in[...]
    vh[0] = vv_in[...]
    vh[1] = hv_in[...]


def pack_outer_kernel(idx, o_in, oo_in, o, oo):
    o[...] = o_in[...]
    oo[...] = oo_in[...]


def side_inverse_kernel(own, beside, across, out):
    mats = []
    first = own[...] + beside[...]
    for full in (first, across[...]):
        n = full.shape[0] // B
        mats.append(
            {
                (i, j): full[i * B : (i + 1) * B, j * B : (j + 1) * B]
                for i in range(n)
                for j in range(n)
            }
        )
    for index, result in enumerate(block_inverse(mats, n)):
        for (i, j), value in result.items():
            out[index, i * B : (i + 1) * B, j * B : (j + 1) * B] = value


def schur_inverse_kernel(sides, vh, vh_y, from_x, u_out, s_out, schur):
    e = vh.shape[1]
    u = []
    c = []
    c.append(jnp.concatenate([vh[1], from_x[1]], axis=1))
    c.append(jnp.concatenate([vh_y[1], from_x[2]], axis=1))
    for k in range(2):
        value = dot_full(sides[k], c[k])
        u_out[k] = value
        u.append(value)
    total = jnp.dot(
        jnp.concatenate([c[0], c[1]], axis=0).T,
        jnp.concatenate(u, axis=0),
        precision=lax.Precision.HIGHEST,
        preferred_element_type=F32,
    )
    schur[...] = -total
    schur[:e, :e] += vh[0] + vh_y[0]
    schur[e:, e:] += from_x[0]
    n = 2 * e // B
    mat = {
        (i, j): schur[i * B : (i + 1) * B, j * B : (j + 1) * B] for i in range(n) for j in range(n)
    }
    (result,) = block_inverse([mat], n)
    for (i, j), value in result.items():
        s_out[i * B : (i + 1) * B, j * B : (j + 1) * B] = value


def quarter_kernel(
    idx, o, o_x, o_y, late, oo, sides, u, s_inv, out, pc_hi, pc_lo, s_hi, s_lo, h_hi, h_lo, u_hi, u_lo
):
    e = o.shape[0] // 2
    g = pl.program_id(0)
    x = idx[0]
    same = idx[4]
    r = g // 2

    def place(c):
        return x if c == 0 else 1 - x

    def fill(first, second, k):
        pair = split(u[k])
        for c, source in enumerate((first, second)):
            oh = source[:, :e]
            oh_pair = split(oh)
            value = -dot_split(oh_pair, pair)
            halves = [value[:, :e], value[:, e:]]
            halves[c] = halves[c] + source[:, e:]
            for part in range(2):
                start = pl.multiple_of((2 * part + place(c)) * e, e)
                rows = pl.ds(start, e)
                for q in range(2):
                    hi, lo = split(halves[q][part * e : (part + 1) * e, :])
                    pc_hi[rows, q * e : (q + 1) * e] = hi
                    pc_lo[rows, q * e : (q + 1) * e] = lo
                pc_hi[rows, 2 * e :] = oh_pair[0][part * e : (part + 1) * e, :]
                pc_lo[rows, 2 * e :] = oh_pair[1][part * e : (part + 1) * e, :]

    @pl.when(g == 0)
    def _():
        s_hi[...], s_lo[...] = split(s_inv[...])
        h_hi[...], h_lo[...] = split(sides[0])
        u_hi[...], u_lo[...] = split(u[0])

    @pl.when((g == 0) & (same == 1))
    def _():
        fill(o, o_x, 0)

    @pl.when((g == 0) & (same == 0))
    def _():
        fill(o_y, late, 1)

    part = pl.ds(pl.multiple_of((g % 2) * e, e), e)
    rows = jnp.where(r == 0, o[part, :], o_x[part, :])
    oh = split(rows[:, :e])
    ov = rows[:, e:]
    base = -dot_split(oh, (u_hi[...], u_lo[...]))
    left = base[:, :e] + jnp.where(r == 0, ov, 0.0)
    right = base[:, e:] + jnp.where(r == 0, 0.0, ov)
    p = split(jnp.concatenate([left, right], axis=1))
    gain = split(dot_split(p, (s_hi[...], s_lo[...])))

    @pl.when(same == 0)
    def _():
        out[...] = -dot_split(gain, (pc_hi[:, : 2 * e], pc_lo[:, : 2 * e]), True)

    @pl.when(same == 1)
    def _():
        side = split(dot_split(oh, (h_hi[...], h_lo[...])))
        both = tuple(jnp.concatenate([gain[k], side[k]], axis=1) for k in range(2))
        out[...] = -dot_split(both, (pc_hi[...], pc_lo[...]), True)
        direct = jnp.where(r == 0, oo[part, :], late[part, :])
        where = jnp.where(r == 0, x, 1 - x)
        for t in range(2):
            cols = pl.ds(pl.multiple_of((2 * t + where) * e, e), e)
            out[:, cols] += direct[:, t * e : (t + 1) * e]


def whole(shape):
    return pl.BlockSpec(shape, lambda *_: (0,) * len(shape))


def body(leaf_maps):
    size = leaf_maps.shape[1]
    e = size // 4
    column_bit = lax.axis_index("gx") // (lax.axis_size("gx") // 2)
    row_bit = lax.axis_index("gy") // (lax.axis_size("gy") // 2)
    far_x = lax.axis_size("gx").bit_length() - 2
    far_y = lax.axis_size("gy").bit_length() - 2
    same = column_bit == row_bit
    idx = jnp.stack(
        [column_bit, 2 + row_bit, 1 - column_bit, 3 - row_bit, same.astype(jnp.int32)]
    ).astype(jnp.int32)
    limit = 56 * 1024 * 1024

    def over_z(value):
        return partner_2(value, "gx", far_x)

    def over_y(value):
        return partner_2(value, "gy", far_y)

    def leaf_block(pick):
        return pl.BlockSpec((None, e, e), pick)

    hh, vh = pl.pallas_call(
        pack_inner_kernel,
        grid_spec=pltpu.PrefetchScalarGridSpec(
            num_scalar_prefetch=1,
            grid=(1,),
            in_specs=[
                leaf_block(lambda i, s: (0, s[2], s[2])),
                leaf_block(lambda i, s: (0, s[3], s[3])),
                leaf_block(lambda i, s: (0, s[2], s[3])),
            ],
            out_specs=[whole((e, e)), whole((2, e, e))],
        ),
        out_shape=[
            jax.ShapeDtypeStruct((e, e), F32),
            jax.ShapeDtypeStruct((2, e, e), F32),
        ],
        name="pack_inner",
    )(idx, leaf_maps, leaf_maps, leaf_maps)
    hh_x = over_z(hh)
    vh_y = over_y(vh)

    o, oo = pl.pallas_call(
        pack_outer_kernel,
        grid_spec=pltpu.PrefetchScalarGridSpec(
            num_scalar_prefetch=1,
            grid=(2, 2),
            in_specs=[
                leaf_block(lambda i, j, s: (0, s[i], s[2 + j])),
                leaf_block(lambda i, j, s: (0, s[i], s[j])),
            ],
            out_specs=[pl.BlockSpec((e, e), lambda i, j, s: (i, j))] * 2,
        ),
        out_shape=[jax.ShapeDtypeStruct((2 * e, 2 * e), F32)] * 2,
        name="pack_outer",
    )(idx, leaf_maps, leaf_maps)

    hh_sum = over_y(hh + hh_x)
    o_for_z, _ = lax.optimization_barrier((o, hh_x))
    o_x = over_z(o_for_z)
    from_x = over_z(jnp.stack([vh[0] + vh_y[0], vh[1], vh_y[1]]))
    o_for_y, _ = lax.optimization_barrier((o, vh_y))
    o_y = over_y(o_for_y)
    late = over_z(jnp.where(same, o_y, oo))

    sides = pl.pallas_call(
        side_inverse_kernel,
        out_shape=jax.ShapeDtypeStruct((2, e, e), F32),
        compiler_params=pltpu.CompilerParams(vmem_limit_bytes=limit),
        cost_estimate=pl.CostEstimate(flops=20_000_000_000, bytes_accessed=2**20, transcendentals=0),
        name="side_inverse",
    )(hh, hh_x, hh_sum)

    u, s_inv = pl.pallas_call(
        schur_inverse_kernel,
        out_shape=[
            jax.ShapeDtypeStruct((2, e, 2 * e), F32),
            jax.ShapeDtypeStruct((2 * e, 2 * e), F32),
        ],
        scratch_shapes=[pltpu.VMEM((2 * e, 2 * e), F32)],
        compiler_params=pltpu.CompilerParams(vmem_limit_bytes=limit),
        cost_estimate=pl.CostEstimate(flops=35_000_000_000, bytes_accessed=2**21, transcendentals=0),
        name="schur_inverse",
    )(sides, vh, vh_y, from_x)

    half = (2 * e, 2 * e)

    def out_pick(g, s):
        r = g // 2
        return (0, 2 * (g % 2) + (1 - r) * s[0] + r * (1 - s[0]), 0)

    return pl.pallas_call(
        quarter_kernel,
        grid_spec=pltpu.PrefetchScalarGridSpec(
            num_scalar_prefetch=1,
            grid=(4,),
            in_specs=[whole(half)] * 5
            + [whole((2, e, e)), whole((2, e, 2 * e)), whole(half)],
            out_specs=pl.BlockSpec((None, e, size), out_pick),
            scratch_shapes=[
                pltpu.VMEM((size, 3 * e), BF16),
                pltpu.VMEM((size, 3 * e), BF16),
                pltpu.VMEM(half, BF16),
                pltpu.VMEM(half, BF16),
                pltpu.VMEM((e, e), BF16),
                pltpu.VMEM((e, e), BF16),
                pltpu.VMEM((e, 2 * e), BF16),
                pltpu.VMEM((e, 2 * e), BF16),
            ],
        ),
        out_shape=jax.ShapeDtypeStruct((1, size, size), F32),
        compiler_params=pltpu.CompilerParams(vmem_limit_bytes=limit),
        cost_estimate=pl.CostEstimate(flops=9_000_000_000, bytes_accessed=2**23, transcendentals=0),
        name="quarter",
    )(idx, o, o_x, o_y, late, oo, sides, u, s_inv)


def solution(mesh):
    return jax.shard_map(
        body,
        mesh=mesh,
        in_specs=(P(None, "gy", "gx"),),
        out_specs=P(None, "gy", "gx"),
        check_vma=False,
    )
```

```python
import functools

import jax
import jax.numpy as jnp
from jax import lax
from jax.experimental import pallas as pl
from jax.experimental.pallas import tpu as pltpu
from jax.sharding import PartitionSpec as P

F32 = jnp.float32
BF16 = jnp.bfloat16
B = 128
W = 4


def solve_4(s, x):
    a0, a1, a2 = s[0, 0], s[1, 0], s[1, 1]
    b = [[s[2, 0], s[2, 1]], [s[3, 0], s[3, 1]]]
    r = 1.0 / (a0 * a2 - a1 * a1)
    e = [[b[i][0] * a2 - b[i][1] * a1, b[i][1] * a0 - b[i][0] * a1] for i in range(2)]
    f00 = e[0][0] * b[0][0] + e[0][1] * b[0][1]
    f10 = e[1][0] * b[0][0] + e[1][1] * b[0][1]
    f11 = e[1][0] * b[1][0] + e[1][1] * b[1][1]
    s0, s1, s2 = s[2, 2] - f00 * r, s[3, 2] - f10 * r, s[3, 3] - f11 * r
    q = 1.0 / (s0 * s2 - s1 * s1)
    t = [[e[i][j] * r for j in range(2)] for i in range(2)]
    y = [x[2 + i] - (t[i][0] * x[0] + t[i][1] * x[1]) for i in range(2)]
    w = [(a2 * x[0] - a1 * x[1]) * r, (a0 * x[1] - a1 * x[0]) * r]
    high = [(s2 * y[0] - s1 * y[1]) * q, (s0 * y[1] - s1 * y[0]) * q]
    low = [w[j] - (t[0][j] * high[0] + t[1][j] * high[1]) for j in range(2)]
    return low + high


def sweep(mats):
    lane_8 = lax.broadcasted_iota(jnp.int32, (8, B), 1)
    lane = lax.broadcasted_iota(jnp.int32, (B, B), 1)
    sub = lax.broadcasted_iota(jnp.int32, (B, B), 0)
    mats = list(mats)
    for k in range(0, B, W):
        inside_8 = (lane_8 >= k) & (lane_8 < k + W)
        below = (sub >= k) & (sub < k + W)
        inside = ((lane >= k) & (lane < k + W)) | below
        rows = [[jnp.broadcast_to(a[k + j : k + j + 1, :], (8, B)) for j in range(W)] for a in mats]
        s = [
            {
                (i, j): jnp.broadcast_to(row[j][:, k + i : k + i + 1], (8, B))
                for i in range(W)
                for j in range(i + 1)
            }
            for row in rows
        ]
        cols = [[jnp.broadcast_to(a[:, k + j : k + j + 1], (B, B)) for j in range(W)] for a in mats]
        for m in range(len(mats)):
            x = [
                jnp.where(inside_8, jnp.where(lane_8 == k + j, -1.0, 0.0), rows[m][j])
                for j in range(W)
            ]
            r = [jnp.concatenate([v] * (B // 8), axis=0) for v in solve_4(s[m], x)]
            base = jnp.where(inside, 0.0, mats[m])
            c = [
                jnp.where(below, jnp.where(sub == k + j, -1.0, 0.0), cols[m][j]) for j in range(W)
            ]
            mats[m] = base - ((c[0] * r[0] + c[1] * r[1]) + (c[2] * r[2] + c[3] * r[3]))
    return mats


def dot_full(a, b):
    return jnp.dot(a, b, precision=lax.Precision.HIGHEST, preferred_element_type=F32)


def block_sweep(refs, k):
    at = pl.ds(pl.multiple_of(k * B, B), B)
    swept = sweep([ref[at, at] for ref in refs])
    for ref, minus in zip(refs, swept):
        row = dot_full(-minus, ref[at, :])
        col = ref[:, at]
        ref[...] = ref[...] - dot_full(col, row)
        ref[at, :] = row
        ref[:, at] = dot_full(col, -minus)
        ref[at, at] = minus


def split(x):
    hi = x.astype(BF16)
    return hi, (x - hi.astype(F32)).astype(BF16)


def dot_split(a, b, transposed=False):
    dims = (((1,), (1 if transposed else 0,)), ((), ()))
    one = functools.partial(lax.dot_general, dimension_numbers=dims, preferred_element_type=F32)
    return one(a[0], b[0]) + (one(a[0], b[1]) + one(a[1], b[0]))


MESH = pl.DeviceIdType.MESH


def inverse_kernel(
    leaf,
    o,
    o_x,
    o_y,
    o_d,
    oo,
    oo_x,
    sides,
    u,
    s_inv,
    hh,
    hh_x,
    hh_sum,
    vv,
    hv,
    vv_y,
    hv_y,
    vv_sum,
    vv_x,
    hv_x,
    hv_d,
    local_sem,
    send_sem,
    recv_sem,
):
    e = hh.shape[0]
    nx, ny = lax.axis_size("gx"), lax.axis_size("gy")
    gx, gy = lax.axis_index("gx"), lax.axis_index("gy")
    across, above = lax.rem(gx + nx // 2, nx), lax.rem(gy + ny // 2, ny)
    cb, rb = gx // (nx // 2), gy // (ny // 2)
    mixed = cb != rb
    beside, over, corner = (across, gy), (gx, above), (across, above)

    def place(side):
        return pl.ds(pl.multiple_of(side * e, e), e)

    west, south, h, v = place(cb), place(2 + rb), place(1 - cb), place(3 - rb)

    def local(rows, cols, dst, index):
        return pltpu.make_async_copy(leaf.at[0, rows, cols], dst, local_sem.at[index])

    def send(src, dst, index, device):
        return pltpu.make_async_remote_copy(
            src_ref=src,
            dst_ref=dst,
            send_sem=send_sem.at[index],
            recv_sem=recv_sem.at[index],
            device_id=device,
            device_id_type=MESH,
        )

    first = [local(h, h, hh, 0), local(v, v, vv, 1), local(h, v, hv, 2)]
    rest = [
        local(west, h, o.at[:e, :e], 3),
        local(west, v, o.at[:e, e:], 4),
        local(south, h, o.at[e:, :e], 5),
        local(south, v, o.at[e:, e:], 6),
        local(west, west, oo.at[0], 7),
        local(west, south, oo.at[1], 8),
        local(south, south, oo.at[2], 9),
    ]
    for copy in first:
        copy.start()
    for copy in rest:
        copy.start()

    barrier = pltpu.get_barrier_semaphore()
    for device in (beside, over, corner):
        pl.semaphore_signal(barrier, inc=1, device_id=device, device_id_type=MESH)
    pl.semaphore_wait(barrier, 3)

    send_hh = send(hh, hh_x, 0, beside)
    send_vv = send(vv, vv_y, 1, over)
    send_hv_y = send(hv, hv_y, 2, over)
    send_hv = send(hv, hv_x, 3, beside)
    send_sum = send(hh_x, hh_sum, 4, over)
    send_vv_sum = send(vv_sum, vv_x, 5, beside)
    send_hv_d = send(hv_x, hv_d, 6, over)
    send_o_x = send(o, o_x, 7, beside)
    send_o_y = send(o, o_y, 8, over)
    send_o_d = send(o, o_d, 9, corner)
    send_oo = send(oo, oo_x, 10, beside)

    first[0].wait()
    send_hh.start()
    first[1].wait()
    send_vv.start()
    first[2].wait()
    send_hv_y.start()
    send_hh.wait_recv()
    hh_x[...] += hh[...]
    send_sum.start()
    send_hv.start()
    send_vv.wait_recv()
    vv_sum[...] = vv[...] + vv_y[...]
    send_vv_sum.start()
    for copy in rest:
        copy.wait()
    send_hv.wait_recv()
    send_hv_d.start()
    send_o_x.start()

    @pl.when(jnp.logical_not(mixed))
    def _():
        send_o_y.start()

    sides[0] = hh_x[...]
    send_sum.wait_recv()
    sides[1] = hh_sum[...]
    block_sweep([sides.at[0], sides.at[1]], 0)

    @pl.when(mixed)
    def _():
        send_o_d.start()
        send_oo.start()

    block_sweep([sides.at[0], sides.at[1]], 1)
    sides[...] = -sides[...]

    send_hv_y.wait_recv()
    send_hv_d.wait_recv()
    send_vv_sum.wait_recv()
    c = [
        jnp.concatenate([hv[...], hv_x[...]], axis=1),
        jnp.concatenate([hv_y[...], hv_d[...]], axis=1),
    ]
    for k in range(2):
        u[k] = dot_full(sides[k], c[k])
    both = jnp.concatenate(c, axis=0)
    s_inv[...] = -dot_full(both.T, jnp.concatenate([u[0], u[1]], axis=0))
    s_inv[:e, :e] += vv_sum[...]
    s_inv[e:, e:] += vv_x[...]

    @pl.loop(0, 2 * e // B)
    def _(k):
        block_sweep([s_inv], k)

    s_inv[...] = -s_inv[...]

    @pl.when(mixed)
    def _():
        send_o_y.wait_recv()
        send_o_d.wait()
        send_oo.wait_send()

    @pl.when(jnp.logical_not(mixed))
    def _():
        send_o_y.wait_send()
        send_oo.wait_recv()

    send_o_x.wait()
    for copy in (send_hh, send_vv, send_hv_y, send_hv, send_sum, send_vv_sum, send_hv_d):
        copy.wait_send()


def quarter_kernel(
    idx, o, o_x, o_y, o_d, oo, oo_x, sides, u, s_inv, out, pc_hi, pc_lo, s_hi, s_lo, h_hi, h_lo, u_hi, u_lo
):
    e = o.shape[0] // 2
    g = pl.program_id(0)
    x = idx[0]
    same = idx[4]
    r = g // 2

    def place(c):
        return x if c == 0 else 1 - x

    def fill(first, second, k):
        pair = split(u[k])
        for c, source in enumerate((first, second)):
            oh = source[:, :e]
            oh_pair = split(oh)
            value = -dot_split(oh_pair, pair)
            halves = [value[:, :e], value[:, e:]]
            halves[c] = halves[c] + source[:, e:]
            for part in range(2):
                start = pl.multiple_of((2 * part + place(c)) * e, e)
                rows = pl.ds(start, e)
                for q in range(2):
                    hi, lo = split(halves[q][part * e : (part + 1) * e, :])
                    pc_hi[rows, q * e : (q + 1) * e] = hi
                    pc_lo[rows, q * e : (q + 1) * e] = lo
                pc_hi[rows, 2 * e :] = oh_pair[0][part * e : (part + 1) * e, :]
                pc_lo[rows, 2 * e :] = oh_pair[1][part * e : (part + 1) * e, :]

    @pl.when(g == 0)
    def _():
        s_hi[...], s_lo[...] = split(s_inv[...])
        h_hi[...], h_lo[...] = split(sides[0])
        u_hi[...], u_lo[...] = split(u[0])

    @pl.when((g == 0) & (same == 1))
    def _():
        fill(o, o_x, 0)

    @pl.when((g == 0) & (same == 0))
    def _():
        fill(o_y, o_d, 1)

    part = pl.ds(pl.multiple_of((g % 2) * e, e), e)
    rows = jnp.where(r == 0, o[part, :], o_x[part, :])
    oh = split(rows[:, :e])
    ov = rows[:, e:]
    base = -dot_split(oh, (u_hi[...], u_lo[...]))
    left = base[:, :e] + jnp.where(r == 0, ov, 0.0)
    right = base[:, e:] + jnp.where(r == 0, 0.0, ov)
    p = split(jnp.concatenate([left, right], axis=1))
    gain = split(dot_split(p, (s_hi[...], s_lo[...])))

    @pl.when(same == 0)
    def _():
        out[...] = -dot_split(gain, (pc_hi[:, : 2 * e], pc_lo[:, : 2 * e]), True)

    @pl.when(same == 1)
    def _():
        side = split(dot_split(oh, (h_hi[...], h_lo[...])))
        both = tuple(jnp.concatenate([gain[k], side[k]], axis=1) for k in range(2))
        out[...] = -dot_split(both, (pc_hi[...], pc_lo[...]), True)
        where = jnp.where(r == 0, x, 1 - x)
        first = pl.ds(pl.multiple_of(where * e, e), e)
        second = pl.ds(pl.multiple_of((2 + where) * e, e), e)

        @pl.when(g % 2 == 0)
        def _():
            out[:, first] += jnp.where(r == 0, oo[0], oo_x[0])
            out[:, second] += jnp.where(r == 0, oo[1], oo_x[1])

        @pl.when(g % 2 == 1)
        def _():
            out[:, first] += jnp.where(r == 0, oo[1], oo_x[1]).T
            out[:, second] += jnp.where(r == 0, oo[2], oo_x[2])


def in_vmem(count):
    return [pl.BlockSpec(memory_space=pltpu.VMEM)] * count


def body(leaf_maps):
    size = leaf_maps.shape[1]
    e = size // 4
    column_bit = lax.axis_index("gx") // (lax.axis_size("gx") // 2)
    row_bit = lax.axis_index("gy") // (lax.axis_size("gy") // 2)
    same = column_bit == row_bit
    idx = jnp.stack(
        [column_bit, 2 + row_bit, 1 - column_bit, 3 - row_bit, same.astype(jnp.int32)]
    ).astype(jnp.int32)
    limit = 32 * 1024 * 1024
    half = (2 * e, 2 * e)
    block = pltpu.VMEM((e, e), F32)

    o, o_x, o_y, o_d, oo, oo_x, sides, u, s_inv = pl.pallas_call(
        inverse_kernel,
        in_specs=[pl.BlockSpec(memory_space=pltpu.HBM)],
        out_specs=in_vmem(9),
        out_shape=[jax.ShapeDtypeStruct(half, F32)] * 4
        + [jax.ShapeDtypeStruct((3, e, e), F32)] * 2
        + [
            jax.ShapeDtypeStruct((2, e, e), F32),
            jax.ShapeDtypeStruct((2, e, 2 * e), F32),
            jax.ShapeDtypeStruct(half, F32),
        ],
        scratch_shapes=[block] * 11
        + [
            pltpu.SemaphoreType.DMA((10,)),
            pltpu.SemaphoreType.DMA((11,)),
            pltpu.SemaphoreType.DMA((11,)),
        ],
        compiler_params=pltpu.CompilerParams(
            vmem_limit_bytes=limit, collective_id=0, has_side_effects=True
        ),
        cost_estimate=pl.CostEstimate(
            flops=4_000_000_000, bytes_accessed=12 * 2**20, transcendentals=0
        ),
        name="inverse",
    )(leaf_maps)

    def out_pick(g, s):
        r = g // 2
        return (0, 2 * (g % 2) + (1 - r) * s[0] + r * (1 - s[0]), 0)

    return pl.pallas_call(
        quarter_kernel,
        grid_spec=pltpu.PrefetchScalarGridSpec(
            num_scalar_prefetch=1,
            grid=(4,),
            in_specs=in_vmem(9),
            out_specs=pl.BlockSpec((None, e, size), out_pick),
            scratch_shapes=[
                pltpu.VMEM((size, 3 * e), BF16),
                pltpu.VMEM((size, 3 * e), BF16),
                pltpu.VMEM(half, BF16),
                pltpu.VMEM(half, BF16),
                pltpu.VMEM((e, e), BF16),
                pltpu.VMEM((e, e), BF16),
                pltpu.VMEM((e, 2 * e), BF16),
                pltpu.VMEM((e, 2 * e), BF16),
            ],
        ),
        out_shape=jax.ShapeDtypeStruct((1, size, size), F32),
        compiler_params=pltpu.CompilerParams(vmem_limit_bytes=limit),
        cost_estimate=pl.CostEstimate(flops=9_000_000_000, bytes_accessed=2**23, transcendentals=0),
        name="quarter",
    )(idx, o, o_x, o_y, o_d, oo, oo_x, sides, u, s_inv)


def solution(mesh):
    return jax.shard_map(
        body,
        mesh=mesh,
        in_specs=(P(None, "gy", "gx"),),
        out_specs=P(None, "gy", "gx"),
        check_vma=False,
    )
```

```python
import functools

import jax
import jax.numpy as jnp
from jax import lax
from jax.experimental import pallas as pl
from jax.experimental.pallas import tpu as pltpu
from jax.sharding import PartitionSpec as P

F32 = jnp.float32
BF16 = jnp.bfloat16
B = 128
W = 4


def solve_4(s, x):
    a0, a1, a2 = s[0, 0], s[1, 0], s[1, 1]
    b = [[s[2, 0], s[2, 1]], [s[3, 0], s[3, 1]]]
    r = 1.0 / (a0 * a2 - a1 * a1)
    e = [[b[i][0] * a2 - b[i][1] * a1, b[i][1] * a0 - b[i][0] * a1] for i in range(2)]
    f00 = e[0][0] * b[0][0] + e[0][1] * b[0][1]
    f10 = e[1][0] * b[0][0] + e[1][1] * b[0][1]
    f11 = e[1][0] * b[1][0] + e[1][1] * b[1][1]
    s0, s1, s2 = s[2, 2] - f00 * r, s[3, 2] - f10 * r, s[3, 3] - f11 * r
    q = 1.0 / (s0 * s2 - s1 * s1)
    t = [[e[i][j] * r for j in range(2)] for i in range(2)]
    y = [x[2 + i] - (t[i][0] * x[0] + t[i][1] * x[1]) for i in range(2)]
    w = [(a2 * x[0] - a1 * x[1]) * r, (a0 * x[1] - a1 * x[0]) * r]
    high = [(s2 * y[0] - s1 * y[1]) * q, (s0 * y[1] - s1 * y[0]) * q]
    low = [w[j] - (t[0][j] * high[0] + t[1][j] * high[1]) for j in range(2)]
    return low + high


def sweep(mats):
    lane_8 = lax.broadcasted_iota(jnp.int32, (8, B), 1)
    lane = lax.broadcasted_iota(jnp.int32, (B, B), 1)
    sub = lax.broadcasted_iota(jnp.int32, (B, B), 0)
    mats = list(mats)
    for k in range(0, B, W):
        inside_8 = (lane_8 >= k) & (lane_8 < k + W)
        below = (sub >= k) & (sub < k + W)
        inside = ((lane >= k) & (lane < k + W)) | below
        rows = [[jnp.broadcast_to(a[k + j : k + j + 1, :], (8, B)) for j in range(W)] for a in mats]
        s = [
            {
                (i, j): jnp.broadcast_to(row[j][:, k + i : k + i + 1], (8, B))
                for i in range(W)
                for j in range(i + 1)
            }
            for row in rows
        ]
        cols = [[jnp.broadcast_to(a[:, k + j : k + j + 1], (B, B)) for j in range(W)] for a in mats]
        for m in range(len(mats)):
            x = [
                jnp.where(inside_8, jnp.where(lane_8 == k + j, -1.0, 0.0), rows[m][j])
                for j in range(W)
            ]
            r = [jnp.concatenate([v] * (B // 8), axis=0) for v in solve_4(s[m], x)]
            base = jnp.where(inside, 0.0, mats[m])
            c = [
                jnp.where(below, jnp.where(sub == k + j, -1.0, 0.0), cols[m][j]) for j in range(W)
            ]
            mats[m] = base - ((c[0] * r[0] + c[1] * r[1]) + (c[2] * r[2] + c[3] * r[3]))
    return mats


def split(x):
    hi = x.astype(BF16)
    return hi, (x - hi.astype(F32)).astype(BF16)


def left_parts(pair):
    return jnp.concatenate([pair[0], pair[0], pair[1]], axis=1)


def right_parts(pair):
    return jnp.concatenate([pair[0], pair[1], pair[0]], axis=0)


def dot_parts(a, b):
    return jnp.dot(a, b, preferred_element_type=F32)


def block_sweep(refs, k):
    at = pl.ds(pl.multiple_of(k * B, B), B)
    swept = sweep([ref[at, at] for ref in refs])
    for ref, minus in zip(refs, swept):
        p = split(-minus)
        col = left_parts(split(ref[:, at]))
        row = dot_parts(left_parts(p), right_parts(split(ref[at, :])))
        ref[...] = ref[...] - dot_parts(col, right_parts(split(row)))
        ref[at, :] = row
        ref[:, at] = dot_parts(col, right_parts(p))
        ref[at, at] = minus


def dot_split(a, b, transposed=False):
    dims = (((1,), (1 if transposed else 0,)), ((), ()))
    one = functools.partial(lax.dot_general, dimension_numbers=dims, preferred_element_type=F32)
    return one(a[0], b[0]) + (one(a[0], b[1]) + one(a[1], b[0]))


MESH = pl.DeviceIdType.MESH


def inverse_kernel(
    leaf,
    o,
    o_x,
    o_y,
    o_d,
    oo,
    oo_x,
    sides,
    u,
    s_inv,
    hh,
    hh_x,
    vv,
    hv,
    vv_y,
    hv_y,
    vv_sum,
    vv_x,
    hv_x,
    hv_d,
    local_sem,
    send_sem,
    recv_sem,
):
    e = hh.shape[0]
    nx, ny = lax.axis_size("gx"), lax.axis_size("gy")
    gx, gy = lax.axis_index("gx"), lax.axis_index("gy")
    across, above = lax.rem(gx + nx // 2, nx), lax.rem(gy + ny // 2, ny)
    cb, rb = gx // (nx // 2), gy // (ny // 2)
    mixed = cb != rb
    beside, over, corner = (across, gy), (gx, above), (across, above)

    def place(side):
        return pl.ds(pl.multiple_of(side * e, e), e)

    west, south, h, v = place(cb), place(2 + rb), place(1 - cb), place(3 - rb)

    def local(rows, cols, dst, index):
        return pltpu.make_async_copy(leaf.at[0, rows, cols], dst, local_sem.at[index])

    def send(src, dst, index, device):
        return pltpu.make_async_remote_copy(
            src_ref=src,
            dst_ref=dst,
            send_sem=send_sem.at[index],
            recv_sem=recv_sem.at[index],
            device_id=device,
            device_id_type=MESH,
        )

    first = [local(h, h, hh, 0), local(v, v, vv, 1), local(h, v, hv, 2)]
    rest = [
        local(west, h, o.at[:e, :e], 3),
        local(west, v, o.at[:e, e:], 4),
        local(south, h, o.at[e:, :e], 5),
        local(south, v, o.at[e:, e:], 6),
        local(west, west, oo.at[0], 7),
        local(west, south, oo.at[1], 8),
        local(south, south, oo.at[2], 9),
    ]
    for copy in first:
        copy.start()
    for copy in rest:
        copy.start()

    barrier = pltpu.get_barrier_semaphore()
    for device in (beside, over, corner):
        pl.semaphore_signal(barrier, inc=1, device_id=device, device_id_type=MESH)
    pl.semaphore_wait(barrier, 3)

    send_hh = send(hh, hh_x, 0, beside)
    send_vv = send(vv, vv_y, 1, over)
    send_hv_y = send(hv, hv_y, 2, over)
    send_hv = send(hv, hv_x, 3, beside)
    send_side = send(sides.at[0], sides.at[1], 4, over)
    send_vv_sum = send(vv_sum, vv_x, 5, beside)
    send_hv_d = send(hv_x, hv_d, 6, over)
    send_o_x = send(o, o_x, 7, beside)
    send_o_y = send(o, o_y, 8, over)
    send_o_d = send(o.at[:e, :], o_d.at[:e, :], 9, corner)
    send_oo = send(oo, oo_x, 10, beside)
    pass_o_d = send(o_x.at[e:, :], o_d.at[e:, :], 11, over)

    first[0].wait()
    send_hh.start()
    first[1].wait()
    send_vv.start()
    first[2].wait()
    send_hv_y.start()
    send_hh.wait_recv()
    send_hv.start()
    sides[0] = hh[...] + hh_x[...]
    block_sweep([sides.at[0]], 0)
    send_vv.wait_recv()
    vv_sum[...] = vv[...] + vv_y[...]
    send_vv_sum.start()
    send_hv.wait_recv()
    send_hv_d.start()
    block_sweep([sides.at[0]], 1)
    sides[0] = -sides[0]
    send_side.start()
    for copy in rest:
        copy.wait()
    send_o_x.start()

    def couple(k, near, far):
        c = jnp.concatenate([near[...], far[...]], axis=1)
        c_pair = split(c)
        value = dot_parts(left_parts(split(sides[k])), right_parts(c_pair))
        u[k] = value
        u_parts = right_parts(split(value))
        c_parts = jnp.concatenate([c_pair[0].T, c_pair[0].T, c_pair[1].T], axis=1)
        return dot_parts(c_parts, u_parts)

    s_inv[...] = -couple(0, hv, hv_x)
    send_hv_y.wait_recv()
    send_vv_sum.wait_recv()
    s_inv[:e, :e] += vv_sum[...]
    s_inv[e:, e:] += vv_x[...]
    send_hv_d.wait_recv()
    send_side.wait_recv()

    @pl.when(mixed)
    def _():
        send_o_d.start()
        send_oo.start()

    @pl.when(jnp.logical_not(mixed))
    def _():
        send_o_y.start()

    s_inv[...] -= couple(1, hv_y, hv_d)

    @pl.loop(0, 2 * e // B)
    def _(k):
        block_sweep([s_inv], k)

        @pl.when(k == e // B)
        def _():
            send_o_x.wait_recv()

            @pl.when(jnp.logical_not(mixed))
            def _():
                pass_o_d.start()

    s_inv[...] = -s_inv[...]

    @pl.when(mixed)
    def _():
        send_o_y.wait_recv()
        pass_o_d.wait_recv()
        send_o_d.wait()
        send_oo.wait_send()

    @pl.when(jnp.logical_not(mixed))
    def _():
        send_o_y.wait_send()
        pass_o_d.wait_send()
        send_oo.wait_recv()

    for copy in (send_hh, send_vv, send_hv_y, send_hv, send_side, send_vv_sum, send_hv_d, send_o_x):
        copy.wait_send()


def quarter_kernel(
    idx, o, o_x, o_y, o_d, oo, oo_x, sides, u, s_inv, out, pc_hi, pc_lo, s_hi, s_lo, h_hi, h_lo, u_hi, u_lo
):
    e = o.shape[0] // 2
    g = pl.program_id(0)
    x = idx[0]
    same = idx[4]
    r = g // 2

    def place(c):
        return x if c == 0 else 1 - x

    def fill(first, second, k):
        pair = split(u[k])
        for c, source in enumerate((first, second)):
            oh = source[:, :e]
            oh_pair = split(oh)
            value = -dot_split(oh_pair, pair)
            halves = [value[:, :e], value[:, e:]]
            halves[c] = halves[c] + source[:, e:]
            for part in range(2):
                start = pl.multiple_of((2 * part + place(c)) * e, e)
                rows = pl.ds(start, e)
                for q in range(2):
                    hi, lo = split(halves[q][part * e : (part + 1) * e, :])
                    pc_hi[rows, q * e : (q + 1) * e] = hi
                    pc_lo[rows, q * e : (q + 1) * e] = lo
                pc_hi[rows, 2 * e :] = oh_pair[0][part * e : (part + 1) * e, :]
                pc_lo[rows, 2 * e :] = oh_pair[1][part * e : (part + 1) * e, :]

    @pl.when(g == 0)
    def _():
        s_hi[...], s_lo[...] = split(s_inv[...])
        h_hi[...], h_lo[...] = split(sides[0])
        u_hi[...], u_lo[...] = split(u[0])

    @pl.when((g == 0) & (same == 1))
    def _():
        fill(o, o_x, 0)

    @pl.when((g == 0) & (same == 0))
    def _():
        fill(o_y, o_d, 1)

    part = pl.ds(pl.multiple_of((g % 2) * e, e), e)
    rows = jnp.where(r == 0, o[part, :], o_x[part, :])
    oh = split(rows[:, :e])
    ov = rows[:, e:]
    base = -dot_split(oh, (u_hi[...], u_lo[...]))
    left = base[:, :e] + jnp.where(r == 0, ov, 0.0)
    right = base[:, e:] + jnp.where(r == 0, 0.0, ov)
    p = split(jnp.concatenate([left, right], axis=1))
    gain = split(dot_split(p, (s_hi[...], s_lo[...])))

    @pl.when(same == 0)
    def _():
        out[...] = -dot_split(gain, (pc_hi[:, : 2 * e], pc_lo[:, : 2 * e]), True)

    @pl.when(same == 1)
    def _():
        side = split(dot_split(oh, (h_hi[...], h_lo[...])))
        both = tuple(jnp.concatenate([gain[k], side[k]], axis=1) for k in range(2))
        out[...] = -dot_split(both, (pc_hi[...], pc_lo[...]), True)
        where = jnp.where(r == 0, x, 1 - x)
        first = pl.ds(pl.multiple_of(where * e, e), e)
        second = pl.ds(pl.multiple_of((2 + where) * e, e), e)

        @pl.when(g % 2 == 0)
        def _():
            out[:, first] += jnp.where(r == 0, oo[0], oo_x[0])
            out[:, second] += jnp.where(r == 0, oo[1], oo_x[1])

        @pl.when(g % 2 == 1)
        def _():
            out[:, first] += jnp.where(r == 0, oo[1], oo_x[1]).T
            out[:, second] += jnp.where(r == 0, oo[2], oo_x[2])


def in_vmem(count):
    return [pl.BlockSpec(memory_space=pltpu.VMEM)] * count


def body(leaf_maps):
    size = leaf_maps.shape[1]
    e = size // 4
    column_bit = lax.axis_index("gx") // (lax.axis_size("gx") // 2)
    row_bit = lax.axis_index("gy") // (lax.axis_size("gy") // 2)
    same = column_bit == row_bit
    idx = jnp.stack(
        [column_bit, 2 + row_bit, 1 - column_bit, 3 - row_bit, same.astype(jnp.int32)]
    ).astype(jnp.int32)
    limit = 32 * 1024 * 1024
    half = (2 * e, 2 * e)
    block = pltpu.VMEM((e, e), F32)

    o, o_x, o_y, o_d, oo, oo_x, sides, u, s_inv = pl.pallas_call(
        inverse_kernel,
        in_specs=[pl.BlockSpec(memory_space=pltpu.HBM)],
        out_specs=in_vmem(9),
        out_shape=[jax.ShapeDtypeStruct(half, F32)] * 4
        + [jax.ShapeDtypeStruct((3, e, e), F32)] * 2
        + [
            jax.ShapeDtypeStruct((2, e, e), F32),
            jax.ShapeDtypeStruct((2, e, 2 * e), F32),
            jax.ShapeDtypeStruct(half, F32),
        ],
        scratch_shapes=[block] * 10
        + [
            pltpu.SemaphoreType.DMA((10,)),
            pltpu.SemaphoreType.DMA((12,)),
            pltpu.SemaphoreType.DMA((12,)),
        ],
        compiler_params=pltpu.CompilerParams(
            vmem_limit_bytes=limit, collective_id=0, has_side_effects=True
        ),
        cost_estimate=pl.CostEstimate(
            flops=4_000_000_000, bytes_accessed=12 * 2**20, transcendentals=0
        ),
        name="inverse",
    )(leaf_maps)

    def out_pick(g, s):
        r = g // 2
        return (0, 2 * (g % 2) + (1 - r) * s[0] + r * (1 - s[0]), 0)

    return pl.pallas_call(
        quarter_kernel,
        grid_spec=pltpu.PrefetchScalarGridSpec(
            num_scalar_prefetch=1,
            grid=(4,),
            in_specs=in_vmem(9),
            out_specs=pl.BlockSpec((None, e, size), out_pick),
            scratch_shapes=[
                pltpu.VMEM((size, 3 * e), BF16),
                pltpu.VMEM((size, 3 * e), BF16),
                pltpu.VMEM(half, BF16),
                pltpu.VMEM(half, BF16),
                pltpu.VMEM((e, e), BF16),
                pltpu.VMEM((e, e), BF16),
                pltpu.VMEM((e, 2 * e), BF16),
                pltpu.VMEM((e, 2 * e), BF16),
            ],
        ),
        out_shape=jax.ShapeDtypeStruct((1, size, size), F32),
        compiler_params=pltpu.CompilerParams(vmem_limit_bytes=limit),
        cost_estimate=pl.CostEstimate(flops=9_000_000_000, bytes_accessed=2**23, transcendentals=0),
        name="quarter",
    )(idx, o, o_x, o_y, o_d, oo, oo_x, sides, u, s_inv)


def solution(mesh):
    return jax.shard_map(
        body,
        mesh=mesh,
        in_specs=(P(None, "gy", "gx"),),
        out_specs=P(None, "gy", "gx"),
        check_vma=False,
    )
```

```python
import jax
import jax.numpy as jnp
from jax import lax
from jax.experimental import pallas as pl
from jax.experimental.pallas import tpu as pltpu
from jax.sharding import PartitionSpec as P

F32 = jnp.float32
BF16 = jnp.bfloat16
B = 128
W = 4


def solve_4(s, x):
    a0, a1, a2 = s[0, 0], s[1, 0], s[1, 1]
    b = [[s[2, 0], s[2, 1]], [s[3, 0], s[3, 1]]]
    r = 1.0 / (a0 * a2 - a1 * a1)
    e = [[b[i][0] * a2 - b[i][1] * a1, b[i][1] * a0 - b[i][0] * a1] for i in range(2)]
    f00 = e[0][0] * b[0][0] + e[0][1] * b[0][1]
    f10 = e[1][0] * b[0][0] + e[1][1] * b[0][1]
    f11 = e[1][0] * b[1][0] + e[1][1] * b[1][1]
    s0, s1, s2 = s[2, 2] - f00 * r, s[3, 2] - f10 * r, s[3, 3] - f11 * r
    q = 1.0 / (s0 * s2 - s1 * s1)
    t = [[e[i][j] * r for j in range(2)] for i in range(2)]
    y = [x[2 + i] - (t[i][0] * x[0] + t[i][1] * x[1]) for i in range(2)]
    w = [(a2 * x[0] - a1 * x[1]) * r, (a0 * x[1] - a1 * x[0]) * r]
    high = [(s2 * y[0] - s1 * y[1]) * q, (s0 * y[1] - s1 * y[0]) * q]
    low = [w[j] - (t[0][j] * high[0] + t[1][j] * high[1]) for j in range(2)]
    return low + high


def sweep(mats):
    lane_8 = lax.broadcasted_iota(jnp.int32, (8, B), 1)
    lane = lax.broadcasted_iota(jnp.int32, (B, B), 1)
    sub = lax.broadcasted_iota(jnp.int32, (B, B), 0)
    mats = list(mats)
    for k in range(0, B, W):
        inside_8 = (lane_8 >= k) & (lane_8 < k + W)
        below = (sub >= k) & (sub < k + W)
        inside = ((lane >= k) & (lane < k + W)) | below
        rows = [[jnp.broadcast_to(a[k + j : k + j + 1, :], (8, B)) for j in range(W)] for a in mats]
        s = [
            {
                (i, j): jnp.broadcast_to(row[j][:, k + i : k + i + 1], (8, B))
                for i in range(W)
                for j in range(i + 1)
            }
            for row in rows
        ]
        cols = [[jnp.broadcast_to(a[:, k + j : k + j + 1], (B, B)) for j in range(W)] for a in mats]
        for m in range(len(mats)):
            x = [
                jnp.where(inside_8, jnp.where(lane_8 == k + j, -1.0, 0.0), rows[m][j])
                for j in range(W)
            ]
            r = [jnp.concatenate([v] * (B // 8), axis=0) for v in solve_4(s[m], x)]
            base = jnp.where(inside, 0.0, mats[m])
            c = [
                jnp.where(below, jnp.where(sub == k + j, -1.0, 0.0), cols[m][j]) for j in range(W)
            ]
            mats[m] = base - ((c[0] * r[0] + c[1] * r[1]) + (c[2] * r[2] + c[3] * r[3]))
    return mats


def split(x):
    hi = x.astype(BF16)
    return hi, (x - hi.astype(F32)).astype(BF16)


def left_parts(pair):
    return jnp.concatenate([pair[0], pair[0], pair[1]], axis=1)


def right_parts(pair):
    return jnp.concatenate([pair[0], pair[1], pair[0]], axis=0)


def dot_parts(a, b):
    return jnp.dot(a, b, preferred_element_type=F32)


def block_sweep(refs, k):
    at = pl.ds(pl.multiple_of(k * B, B), B)
    swept = sweep([ref[at, at] for ref in refs])
    for ref, minus in zip(refs, swept):
        p = split(-minus)
        col = left_parts(split(ref[:, at]))
        row = dot_parts(left_parts(p), right_parts(split(ref[at, :])))
        ref[...] = ref[...] - dot_parts(col, right_parts(split(row)))
        ref[at, :] = row
        ref[:, at] = dot_parts(col, right_parts(p))
        ref[at, at] = minus


MESH = pl.DeviceIdType.MESH


def inverse_kernel(
    leaf,
    o,
    o_x,
    o_y,
    o_d,
    oo,
    oo_x,
    sides,
    u,
    lhs,
    s_inv,
    hh,
    hh_x,
    vv,
    hv,
    vv_y,
    hv_y,
    vv_sum,
    vv_x,
    hv_x,
    hv_d,
    local_sem,
    send_sem,
    recv_sem,
):
    e = hh.shape[0]
    nx, ny = lax.axis_size("gx"), lax.axis_size("gy")
    gx, gy = lax.axis_index("gx"), lax.axis_index("gy")
    across, above = lax.rem(gx + nx // 2, nx), lax.rem(gy + ny // 2, ny)
    cb, rb = gx // (nx // 2), gy // (ny // 2)
    mixed = cb != rb
    beside, over, corner = (across, gy), (gx, above), (across, above)

    def place(side):
        return pl.ds(pl.multiple_of(side * e, e), e)

    west, south, h, v = place(cb), place(2 + rb), place(1 - cb), place(3 - rb)

    def local(rows, cols, dst, index):
        return pltpu.make_async_copy(leaf.at[0, rows, cols], dst, local_sem.at[index])

    def send(src, dst, index, device):
        return pltpu.make_async_remote_copy(
            src_ref=src,
            dst_ref=dst,
            send_sem=send_sem.at[index],
            recv_sem=recv_sem.at[index],
            device_id=device,
            device_id_type=MESH,
        )

    first = [local(h, h, hh, 0), local(v, v, vv, 1), local(h, v, hv, 2)]
    rest = [
        local(west, h, o.at[:e, :e], 3),
        local(west, v, o.at[:e, e:], 4),
        local(south, h, o.at[e:, :e], 5),
        local(south, v, o.at[e:, e:], 6),
        local(west, west, oo.at[0], 7),
        local(west, south, oo.at[1], 8),
        local(south, south, oo.at[2], 9),
    ]
    for copy in first:
        copy.start()
    for copy in rest:
        copy.start()

    barrier = pltpu.get_barrier_semaphore()
    for device in (beside, over, corner):
        pl.semaphore_signal(barrier, inc=1, device_id=device, device_id_type=MESH)
    pl.semaphore_wait(barrier, 3)

    send_hh = send(hh, hh_x, 0, beside)
    send_vv = send(vv, vv_y, 1, over)
    send_hv_y = send(hv, hv_y, 2, over)
    send_hv = send(hv, hv_x, 3, beside)
    send_side = send(sides.at[0], sides.at[1], 4, over)
    send_vv_sum = send(vv_sum, vv_x, 5, beside)
    send_hv_d = send(hv_x, hv_d, 6, over)
    send_o_x = send(o, o_x, 7, beside)
    send_o_y = send(o, o_y, 8, over)
    send_o_d = send(o.at[:e, :], o_d.at[:e, :], 9, corner)
    send_oo = send(oo, oo_x, 10, beside)
    pass_o_d = send(o_x.at[e:, :], o_d.at[e:, :], 11, over)

    first[0].wait()
    send_hh.start()
    first[1].wait()
    send_vv.start()
    first[2].wait()
    send_hv_y.start()
    send_hh.wait_recv()
    send_hv.start()
    sides[0] = hh[...] + hh_x[...]
    block_sweep([sides.at[0]], 0)
    send_vv.wait_recv()
    vv_sum[...] = vv[...] + vv_y[...]
    send_vv_sum.start()
    send_hv.wait_recv()
    send_hv_d.start()
    block_sweep([sides.at[0]], 1)
    sides[0] = -sides[0]
    send_side.start()
    for copy in rest:
        copy.wait()
    send_o_x.start()

    def couple(k, near, far):
        c = jnp.concatenate([near[...], far[...]], axis=1)
        c_pair = split(c)
        value = dot_parts(left_parts(split(sides[k])), right_parts(c_pair))
        u[k] = value
        u_parts = right_parts(split(value))
        c_parts = jnp.concatenate([c_pair[0].T, c_pair[0].T, c_pair[1].T], axis=1)
        return dot_parts(c_parts, u_parts)

    s_inv[...] = -couple(0, hv, hv_x)
    send_hv_y.wait_recv()
    send_vv_sum.wait_recv()
    s_inv[:e, :e] += vv_sum[...]
    s_inv[e:, e:] += vv_x[...]
    send_hv_d.wait_recv()
    send_side.wait_recv()

    @pl.when(mixed)
    def _():
        send_o_d.start()
        send_oo.start()

    @pl.when(jnp.logical_not(mixed))
    def _():
        send_o_y.start()

    s_inv[...] -= couple(1, hv_y, hv_d)

    @pl.loop(0, 2 * e // B)
    def _(k):
        block_sweep([s_inv], k)

        @pl.when(k == 2)
        def _():
            send_o_x.wait_recv()

            @pl.when(jnp.logical_not(mixed))
            def _():
                pass_o_d.start()

    s_parts = right_parts(split(s_inv[...]))
    uh_parts = jnp.concatenate([right_parts(split(u[0])), right_parts(split(sides[0]))], axis=1)
    for k, source in enumerate((o, o_x)):
        both = dot_parts(left_parts(split(source[:, :e])), uh_parts)
        halves = [-both[:, :e], -both[:, e : 2 * e]]
        halves[k] = halves[k] + source[:, e:]
        p = left_parts(split(jnp.concatenate(halves, axis=1)))
        rows = slice(2 * k * e, 2 * (k + 1) * e)
        lhs[rows, : 6 * e] = left_parts(split(dot_parts(p, s_parts)))
        lhs[rows, 6 * e :] = left_parts(split(-both[:, 2 * e :]))

    @pl.when(mixed)
    def _():
        send_o_y.wait_recv()
        pass_o_d.wait_recv()
        send_o_d.wait()
        send_oo.wait_send()

    @pl.when(jnp.logical_not(mixed))
    def _():
        send_o_y.wait_send()
        pass_o_d.wait_send()
        send_oo.wait_recv()

    for copy in (send_hh, send_vv, send_hv_y, send_hv, send_side, send_vv_sum, send_hv_d, send_o_x):
        copy.wait_send()


def quarter_kernel(idx, o, o_x, o_y, o_d, oo, oo_x, u, lhs, out, pc):
    e = o.shape[0] // 2
    g = pl.program_id(0)
    x = idx[0]
    same = idx[4]
    r = g // 2

    def place(c):
        return x if c == 0 else 1 - x

    def fill(first, second, u_parts):
        for c, source in enumerate((first, second)):
            pair = split(source[:, :e])
            value = -dot_parts(left_parts(pair), u_parts)
            halves = [value[:, :e], value[:, e:]]
            halves[c] = halves[c] + source[:, e:]
            for part in range(2):
                rows = pl.ds(pl.multiple_of((2 * part + place(c)) * e, e), e)
                of = slice(part * e, (part + 1) * e)
                for q in range(2):
                    hi, lo = split(halves[q][of, :])
                    for n, piece in enumerate((hi, lo, hi)):
                        pc[rows, (2 * n + q) * e : (2 * n + q + 1) * e] = piece
                for n, piece in enumerate((pair[0], pair[1], pair[0])):
                    pc[rows, (6 + n) * e : (7 + n) * e] = piece[of, :]

    @pl.when((g == 0) & (same == 1))
    def _():
        fill(o, o_x, right_parts(split(u[0])))

    @pl.when((g == 0) & (same == 0))
    def _():
        fill(o_y, o_d, right_parts(split(u[1])))

    rows = pl.ds(pl.multiple_of(g * e, e), e)

    def times_columns(a, b):
        return lax.dot_general(a, b, (((1,), (1,)), ((), ())), preferred_element_type=F32)

    @pl.when(same == 0)
    def _():
        out[...] = times_columns(lhs[rows, : 6 * e], pc[:, : 6 * e])

    @pl.when(same == 1)
    def _():
        out[...] = times_columns(lhs[rows, :], pc[...])
        where = jnp.where(r == 0, x, 1 - x)
        first = pl.ds(pl.multiple_of(where * e, e), e)
        second = pl.ds(pl.multiple_of((2 + where) * e, e), e)

        @pl.when(g % 2 == 0)
        def _():
            out[:, first] += jnp.where(r == 0, oo[0], oo_x[0])
            out[:, second] += jnp.where(r == 0, oo[1], oo_x[1])

        @pl.when(g % 2 == 1)
        def _():
            out[:, first] += jnp.where(r == 0, oo[1], oo_x[1]).T
            out[:, second] += jnp.where(r == 0, oo[2], oo_x[2])


def in_vmem(count):
    return [pl.BlockSpec(memory_space=pltpu.VMEM)] * count


def body(leaf_maps):
    size = leaf_maps.shape[1]
    e = size // 4
    column_bit = lax.axis_index("gx") // (lax.axis_size("gx") // 2)
    row_bit = lax.axis_index("gy") // (lax.axis_size("gy") // 2)
    same = column_bit == row_bit
    idx = jnp.stack(
        [column_bit, 2 + row_bit, 1 - column_bit, 3 - row_bit, same.astype(jnp.int32)]
    ).astype(jnp.int32)
    limit = 32 * 1024 * 1024
    half = (2 * e, 2 * e)
    block = pltpu.VMEM((e, e), F32)

    o, o_x, o_y, o_d, oo, oo_x, _, u, lhs = pl.pallas_call(
        inverse_kernel,
        in_specs=[pl.BlockSpec(memory_space=pltpu.HBM)],
        out_specs=in_vmem(9),
        out_shape=[jax.ShapeDtypeStruct(half, F32)] * 4
        + [jax.ShapeDtypeStruct((3, e, e), F32)] * 2
        + [
            jax.ShapeDtypeStruct((2, e, e), F32),
            jax.ShapeDtypeStruct((2, e, 2 * e), F32),
            jax.ShapeDtypeStruct((size, 9 * e), BF16),
        ],
        scratch_shapes=[pltpu.VMEM(half, F32)]
        + [block] * 10
        + [
            pltpu.SemaphoreType.DMA((10,)),
            pltpu.SemaphoreType.DMA((12,)),
            pltpu.SemaphoreType.DMA((12,)),
        ],
        compiler_params=pltpu.CompilerParams(
            vmem_limit_bytes=limit, collective_id=0, has_side_effects=True
        ),
        cost_estimate=pl.CostEstimate(
            flops=4_000_000_000, bytes_accessed=12 * 2**20, transcendentals=0
        ),
        name="inverse",
    )(leaf_maps)

    def out_pick(g, s):
        r = g // 2
        return (0, 2 * (g % 2) + (1 - r) * s[0] + r * (1 - s[0]), 0)

    return pl.pallas_call(
        quarter_kernel,
        grid_spec=pltpu.PrefetchScalarGridSpec(
            num_scalar_prefetch=1,
            grid=(4,),
            in_specs=in_vmem(8),
            out_specs=pl.BlockSpec((None, e, size), out_pick),
            scratch_shapes=[
                pltpu.VMEM((size, 9 * e), BF16),
            ],
        ),
        out_shape=jax.ShapeDtypeStruct((1, size, size), F32),
        compiler_params=pltpu.CompilerParams(vmem_limit_bytes=limit),
        cost_estimate=pl.CostEstimate(flops=9_000_000_000, bytes_accessed=2**23, transcendentals=0),
        name="quarter",
    )(idx, o, o_x, o_y, o_d, oo, oo_x, u, lhs)


def solution(mesh):
    return jax.shard_map(
        body,
        mesh=mesh,
        in_specs=(P(None, "gy", "gx"),),
        out_specs=P(None, "gy", "gx"),
        check_vma=False,
    )
```
